32 devices in a mesh: row: 16 (over z, x, core), col: 2 (over y).
Axes of the slice: x: 2, y: 2, z: 4, core: 2. Of those that a mesh axis runs over, the one named last changes fastest.
Arguments:
- inverse_rows: bfloat16 [2048, 2048], P('row', 'col'), may hold values from -6 to 6
- panel_rows: bfloat16 [2048, 512], P('row', 'col'), may hold values from -0.1875 to 0.1875
- diag_inverse: float32 [512, 512], P('row', 'col'), may hold values from -6 to 6
- pattern: int32 [1, 16], replicated, may hold values 0 or 1
Outputs:
- offdiag: bfloat16 [2048, 512], P('row', 'col')
- diag_block: float32 [512, 512], P('row', 'col')
The draws below stay inside these ranges and needn't reach their ends.
All inputs are finite; a program needn't handle non-finite values.
Results may differ from the reference program's by a relative error of at most 0.0018.
Values may be sent and summed in bfloat16 or wider, within the bound.
A program may use at most 64 MiB of HBM per device.

```python
import jax
import jax.numpy as jnp
from jax import lax

BLK = 128
W = 512
NB = 16
NSUP = 1


def plant(entries, stream_key, low, high):
    longest = entries.shape.index(max(entries.shape))
    spots = []
    for shift in (0, 1):
        where = [jax.random.randint(jax.random.fold_in(stream_key, axis), (), 0, length) for axis, length in enumerate(entries.shape)]
        where[longest] = (where[longest] + shift) % entries.shape[longest]
        spots.append(tuple(where))
    return entries.at[spots[0]].set(low).at[spots[1]].set(high)


def shard_levels(rng, extent, cuts, least, largest):
    factor_of, own = 1.0, jax.random.fold_in(rng, 6)
    for dim, blocks in cuts:
        heights = jnp.exp(jax.random.uniform(jax.random.fold_in(own, dim), (blocks,), jnp.float32, least / len(cuts), largest / len(cuts)))
        factor_of = factor_of * jnp.repeat(heights, extent[dim] // blocks).reshape([-1 if axis == dim else 1 for axis in range(len(extent))])
    return factor_of


def bell_draw(stream_key, shape, spread, limit, cuts=(), kind=jnp.bfloat16):
    factor_of = shard_levels(stream_key, shape, cuts, -0.22, 0.18) if cuts else 1.0
    entries = jax.random.normal(stream_key, shape, jnp.float32) * spread * factor_of
    return jnp.minimum(jnp.maximum(entries, -limit), limit).astype(kind)


def setup_inputs(seed: int = 0) -> dict:
    key_list = jax.random.split(jax.random.key(seed), 5)
    return {
        "inverse_rows": bell_draw(key_list[0], (NB * BLK, NB * BLK), 1.0, 6.0, ((0, 16), (1, 2))),
        "panel_rows": bell_draw(key_list[1], (NB * BLK, NSUP * W), (NB * BLK // 2) ** -0.5, 0.1875, ((0, 16), (1, 2))),
        "diag_inverse": bell_draw(key_list[2], (W, NSUP * W), 1.0, 6.0, ((0, 16), (1, 2)), jnp.float32),
        "pattern": plant((jax.random.randint(key_list[3], (NSUP, NB), 0, 2) < 1).astype(jnp.int32), jax.random.fold_in(key_list[3], 1), 0, 1),
    }


def reference(inverse_rows, panel_rows, diag_inverse, pattern):
    live_mask = jnp.repeat(jnp.repeat(pattern.T, BLK, axis=0), W, axis=1) > 0
    masked = jnp.where(live_mask, panel_rows, jnp.zeros_like(panel_rows))
    products = jnp.dot(inverse_rows, masked, preferred_element_type=jnp.float32)
    offdiag = jnp.where(live_mask, -products, jnp.zeros_like(products)).astype(jnp.bfloat16)

    def node_term(index):
        left_block = lax.dynamic_slice_in_dim(masked, index * W, W, 1)
        right_block = lax.dynamic_slice_in_dim(offdiag, index * W, W, 1)
        return lax.dot_general(left_block, right_block, (((0,), (0,)), ((), ())), preferred_element_type=jnp.float32)

    node_terms = lax.map(node_term, jnp.arange(NSUP, dtype=jnp.int32))
    term_cols = jnp.transpose(node_terms, (1, 0, 2)).reshape(W, NSUP * W)
    diag_block = diag_inverse - term_cols
    return offdiag, diag_block
```

```python
import functools

import jax
import jax.numpy as jnp
from jax import lax
from jax.experimental import pallas as pl
from jax.experimental.pallas import tpu as pltpu
from jax.sharding import PartitionSpec as P

MESH = pl.DeviceIdType.MESH
UP, DOWN, ACROSS, PARTNER = range(4)


def kernel(
    rows, cols, group,
    pattern_ref, inv_ref, pan_ref, diag_ref,
    off_ref, out_ref,
    inv_buf, pan_buf, mate, terms, pair_buf, sums, red_buf,
    local_sem, pan_send, pan_recv, inv_send, inv_recv, mate_send, mate_recv,
    pair_send, pair_recv, red_send, red_recv,
):
    row = lax.axis_index("row")
    col = lax.axis_index("col")
    core = row % 2
    side = (row // 2) % 2
    layer = row // 4
    layers = rows // 4
    chips = rows // 2
    chip = row // 2
    partner = row + 1 - 2 * core
    across = row + 2 - 4 * side
    place = col % group
    supernode = col // group
    has_up = layer < layers - 1
    has_down = layer > 0
    height, half = pan_ref.shape

    own_inv = pltpu.make_async_copy(inv_ref, inv_buf.at[col], local_sem.at[0])
    own_pan = pltpu.make_async_copy(pan_ref, pan_buf.at[row], local_sem.at[1])
    own_mate = pltpu.make_async_copy(pan_ref, mate.at[place], local_sem.at[2])
    own_inv.start()
    own_pan.start()
    own_mate.start()

    barrier = pltpu.get_barrier_semaphore()

    def greet(**where):
        pl.semaphore_signal(barrier, inc=1, device_id=where, device_id_type=MESH)

    greet(row=across)
    greet(row=partner)
    for step in range(1, cols):
        greet(col=(col + step) % cols)

    @pl.when(has_up)
    def _():
        greet(row=row + 4)

    @pl.when(has_down)
    def _():
        greet(row=row - 4)

    ends = (layer + layers - 1) // layers + (2 * layers - 2 - layer) // layers
    pl.semaphore_wait(barrier, 2 + cols - 1 + ends)

    pending = []

    def launch(copy, cond=None):
        if cond is None:
            copy.start()
        else:
            pl.when(cond)(copy.start)
        pending.append((cond, copy))

    def panel_copy(source, direction, src=None):
        target = {UP: row + 4, DOWN: row - 4, ACROSS: across, PARTNER: partner}[direction]
        return pltpu.make_async_remote_copy(
            src_ref=pan_buf.at[source] if src is None else src,
            dst_ref=pan_buf.at[source],
            send_sem=pan_send.at[source, direction],
            recv_sem=pan_recv.at[source],
            device_id={"row": target},
            device_id_type=MESH,
        )

    launch(panel_copy(row, ACROSS, pan_ref))
    launch(panel_copy(row, UP, pan_ref), has_up)
    launch(panel_copy(row, DOWN, pan_ref), has_down)
    launch(panel_copy(row, PARTNER, pan_ref))

    inv_copies = []
    for step in range(1, cols):
        copy = pltpu.make_async_remote_copy(
            src_ref=inv_ref,
            dst_ref=inv_buf.at[col],
            send_sem=inv_send.at[step],
            recv_sem=inv_recv.at[step],
            device_id={"col": (col + step) % cols},
            device_id_type=MESH,
        )
        launch(copy)
        inv_copies.append(copy)
    mate_copies = []
    for step in range(1, group):
        copy = pltpu.make_async_remote_copy(
            src_ref=pan_ref,
            dst_ref=mate.at[place],
            send_sem=mate_send.at[step],
            recv_sem=mate_recv.at[step],
            device_id={"col": supernode * group + (place + step) % group},
            device_id_type=MESH,
        )
        launch(copy)
        mate_copies.append(copy)

    def arrive(source, onward, cond=None):
        def take():
            panel_copy(source, PARTNER).wait_recv()

        if cond is None:
            take()
        else:
            pl.when(cond)(take)
        for direction, also in onward:
            both = cond if also is None else (also if cond is None else cond & also)
            launch(panel_copy(source, direction), both)

    def arrive_across(distance):
        if distance == 0:
            arrive(across, [(PARTNER, None)])
        else:
            arrive(across - 4 * distance, [(PARTNER, None)], layer >= distance)
            arrive(across + 4 * distance, [(PARTNER, None)], layer < layers - distance)

    for distance in range(1, layers):
        arrive(
            row - 4 * distance,
            [(UP, has_up), (ACROSS, None), (PARTNER, None)],
            layer >= distance,
        )
        arrive(
            row + 4 * distance,
            [(DOWN, has_down), (ACROSS, None), (PARTNER, None)],
            layer < layers - distance,
        )
        arrive_across(distance - 1)
    arrive_across(layers - 1)

    for index in range(chips):
        panel_copy(2 * index + 1 - core, PARTNER).wait_recv()
    own_inv.wait()
    own_pan.wait()

    per_col = rows // cols
    total = jnp.zeros((height, half), jnp.float32)
    for step in range(cols):
        owner = (col + cols - step) % cols
        if step:
            inv_copies[step - 1].wait_recv()
        parts = []
        for index in range(per_col):
            block = inv_buf[owner, :, index * height : (index + 1) * height]
            live = pattern_ref[supernode, owner * per_col + index] > 0
            parts.append(jnp.where(live, block, jnp.zeros_like(block)))
        panel = pan_buf[pl.ds(owner * per_col, per_col)].reshape(per_col * height, half)
        total += jnp.dot(
            jnp.concatenate(parts, axis=1), panel, preferred_element_type=jnp.float32
        )
    own_live = pattern_ref[supernode, row] > 0
    offdiag = jnp.where(own_live, -total, jnp.zeros_like(total)).astype(jnp.bfloat16)
    off_ref[...] = offdiag

    own_mate.wait()
    for copy in mate_copies:
        copy.wait_recv()
    pairs = chips // group
    for index in range(group):
        term = lax.dot_general(
            mate[index], offdiag, (((0,), (0,)), ((), ())), preferred_element_type=jnp.float32
        )
        terms[index * pairs : (index + 1) * pairs] = term.reshape(pairs, *terms.shape[1:])

    pair_copy = pltpu.make_async_remote_copy(
        src_ref=terms.at[:, 1 - core],
        dst_ref=pair_buf,
        send_sem=pair_send,
        recv_sem=pair_recv,
        device_id={"row": partner},
        device_id_type=MESH,
    )
    launch(pair_copy)
    pair_copy.wait_recv()
    sums[...] = terms[:, core] + pair_buf[...]
    red_copies = []
    for step in range(1, chips):
        target = (chip + step) % chips
        copy = pltpu.make_async_remote_copy(
            src_ref=sums.at[target],
            dst_ref=red_buf.at[chip],
            send_sem=red_send.at[step],
            recv_sem=red_recv.at[step],
            device_id={"row": 2 * target + core},
            device_id_type=MESH,
        )
        launch(copy)
        red_copies.append(copy)
    result = sums[chip]
    for step in range(1, chips):
        red_copies[step - 1].wait_recv()
        result += red_buf[(chip + chips - step) % chips]
    out_ref[...] = diag_ref[...] - result

    for cond, copy in pending:
        if cond is None:
            copy.wait_send()
        else:
            pl.when(cond)(copy.wait_send)


def shards(rows, cols, inverse_rows, panel_rows, diag_inverse, pattern):
    height, half = panel_rows.shape
    chunk = diag_inverse.shape[0]
    group = rows * chunk // half
    chips = rows // 2
    dma = pltpu.SemaphoreType.DMA
    vmem = pl.BlockSpec(memory_space=pltpu.VMEM)
    anywhere = pl.BlockSpec(memory_space=pl.ANY)
    offdiag, diag_block = pl.pallas_call(
        functools.partial(kernel, rows, cols, group),
        out_shape=(
            jax.ShapeDtypeStruct((height, half), jnp.bfloat16),
            jax.ShapeDtypeStruct((chunk, half), jnp.float32),
        ),
        in_specs=[pl.BlockSpec(memory_space=pltpu.SMEM), anywhere, anywhere, vmem],
        out_specs=(vmem, vmem),
        scratch_shapes=[
            pltpu.VMEM((cols, *inverse_rows.shape), jnp.bfloat16),
            pltpu.VMEM((rows, height, half), jnp.bfloat16),
            pltpu.VMEM((group, height, half), jnp.bfloat16),
            pltpu.VMEM((chips, 2, chunk, half), jnp.float32),
            pltpu.VMEM((chips, chunk, half), jnp.float32),
            pltpu.VMEM((chips, chunk, half), jnp.float32),
            pltpu.VMEM((chips, chunk, half), jnp.float32),
            dma((3,)),
            dma((rows, 4)),
            dma((rows,)),
            dma((cols,)),
            dma((cols,)),
            dma((group,)),
            dma((group,)),
            dma,
            dma,
            dma((chips,)),
            dma((chips,)),
        ],
        compiler_params=pltpu.CompilerParams(
            collective_id=0, has_side_effects=True, vmem_limit_bytes=48 * 1024 * 1024
        ),
    )(pattern, inverse_rows, panel_rows, diag_inverse)
    return offdiag, diag_block


def solution(mesh):
    placed = (P("row", "col"), P("row", "col"), P("row", "col"), P())
    return jax.shard_map(
        functools.partial(shards, mesh.shape["row"], mesh.shape["col"]),
        mesh=mesh,
        in_specs=placed,
        out_specs=(P("row", "col"), P("row", "col")),
        check_vma=False,
    )
```

```python
import functools

import jax
import jax.numpy as jnp
from jax import lax
from jax.experimental import pallas as pl
from jax.experimental.pallas import tpu as pltpu
from jax.sharding import PartitionSpec as P

MESH = pl.DeviceIdType.MESH
SPLIT = 1
UP, DOWN, ACROSS, PARTNER = range(4)


def kernel(
    rows, cols, group,
    pattern_hbm, inv_ref, pan_ref, diag_hbm,
    off_ref, out_ref,
    pattern_ref, diag_ref, inv_buf, pan_buf, mate, terms, pair_buf, sums, red_buf,
    local_sem, pan_send, pan_recv, inv_send, inv_recv, mate_send, mate_recv,
    pair_send, pair_recv, red_send, red_recv,
):
    row = lax.axis_index("row")
    col = lax.axis_index("col")
    core = row % 2
    side = (row // 2) % 2
    layer = row // 4
    layers = rows // 4
    chips = rows // 2
    chip = row // 2
    partner = row + 1 - 2 * core
    across = row + 2 - 4 * side
    place = col % group
    supernode = col // group
    has_up = layer < layers - 1
    has_down = layer > 0
    height, half = pan_ref.shape

    own_inv = pltpu.make_async_copy(inv_ref, inv_buf.at[col], local_sem.at[0])
    own_pan = pltpu.make_async_copy(pan_ref, pan_buf.at[row], local_sem.at[1])
    own_mate = pltpu.make_async_copy(pan_ref, mate.at[place], local_sem.at[2])
    own_pattern = pltpu.make_async_copy(pattern_hbm, pattern_ref, local_sem.at[3])
    own_diag = pltpu.make_async_copy(diag_hbm, diag_ref, local_sem.at[4])
    own_pattern.start()
    own_diag.start()
    own_inv.start()
    own_pan.start()
    own_mate.start()

    barrier = pltpu.get_barrier_semaphore()

    def greet(**where):
        pl.semaphore_signal(barrier, inc=1, device_id=where, device_id_type=MESH)

    greet(row=across)
    greet(row=partner)
    for step in range(1, cols):
        greet(col=(col + step) % cols)

    @pl.when(has_up)
    def _():
        greet(row=row + 4)

    @pl.when(has_down)
    def _():
        greet(row=row - 4)

    ends = (layer + layers - 1) // layers + (2 * layers - 2 - layer) // layers
    pl.semaphore_wait(barrier, 2 + cols - 1 + ends)

    pending = []

    def launch(copy, cond=None):
        if cond is None:
            copy.start()
        else:
            pl.when(cond)(copy.start)
        pending.append((cond, copy))

    piece = height // SPLIT

    def panel_copy(source, part, direction, own=False):
        target = {UP: row + 4, DOWN: row - 4, ACROSS: across, PARTNER: partner}[direction]
        lines = pl.ds(part * piece, piece)
        return pltpu.make_async_remote_copy(
            src_ref=pan_ref.at[lines] if own else pan_buf.at[source, lines],
            dst_ref=pan_buf.at[source, lines],
            send_sem=pan_send.at[source, part, direction],
            recv_sem=pan_recv.at[source, part],
            device_id={"row": target},
            device_id_type=MESH,
        )

    for part in range(SPLIT):
        launch(panel_copy(row, part, UP, True), has_up)
        launch(panel_copy(row, part, DOWN, True), has_down)
        launch(panel_copy(row, part, ACROSS, True))
        launch(panel_copy(row, part, PARTNER, True))

    inv_copies = []
    for step in range(1, cols):
        copy = pltpu.make_async_remote_copy(
            src_ref=inv_ref,
            dst_ref=inv_buf.at[col],
            send_sem=inv_send.at[step],
            recv_sem=inv_recv.at[step],
            device_id={"col": (col + step) % cols},
            device_id_type=MESH,
        )
        launch(copy)
        inv_copies.append(copy)
    mate_copies = []
    for step in range(1, group):
        copy = pltpu.make_async_remote_copy(
            src_ref=pan_ref,
            dst_ref=mate.at[place],
            send_sem=mate_send.at[step],
            recv_sem=mate_recv.at[step],
            device_id={"col": supernode * group + (place + step) % group},
            device_id_type=MESH,
        )
        launch(copy)
        mate_copies.append(copy)

    def arrive(source, part, onward, cond=None):
        take = panel_copy(source, part, PARTNER).wait_recv
        if cond is None:
            take()
        else:
            pl.when(cond)(take)
        for direction, also in onward:
            both = cond if also is None else cond & also
            launch(panel_copy(source, part, direction), both)

    for distance in range(1, layers + 1):
        for part in range(SPLIT):
            if distance < layers:
                arrive(
                    row - 4 * distance,
                    part,
                    [(UP, has_up), (ACROSS, None), (PARTNER, None)],
                    layer >= distance,
                )
                arrive(
                    row + 4 * distance,
                    part,
                    [(DOWN, has_down), (ACROSS, None), (PARTNER, None)],
                    layer < layers - distance,
                )
            far = distance - 1
            onward = [(PARTNER, None)]
            if far == 0:
                arrive(across, part, onward)
            else:
                arrive(across - 4 * far, part, onward, layer >= far)
                arrive(across + 4 * far, part, onward, layer < layers - far)

    for index in range(chips):
        for part in range(SPLIT):
            panel_copy(2 * index + 1 - core, part, PARTNER).wait_recv()
    own_pattern.wait()
    own_inv.wait()
    own_pan.wait()

    per_col = rows // cols
    total = jnp.zeros((height, half), jnp.float32)
    for step in range(cols):
        owner = (col + cols - step) % cols
        if step:
            inv_copies[step - 1].wait_recv()
        parts = []
        for index in range(per_col):
            block = inv_buf[owner, :, index * height : (index + 1) * height]
            live = pattern_ref[supernode, owner * per_col + index] > 0
            parts.append(jnp.where(live, block, jnp.zeros_like(block)))
        panel = pan_buf[pl.ds(owner * per_col, per_col)].reshape(per_col * height, half)
        total += jnp.dot(
            jnp.concatenate(parts, axis=1), panel, preferred_element_type=jnp.float32
        )
    own_live = pattern_ref[supernode, row] > 0
    offdiag = jnp.where(own_live, -total, jnp.zeros_like(total)).astype(jnp.bfloat16)
    off_ref[...] = offdiag

    own_mate.wait()
    for copy in mate_copies:
        copy.wait_recv()
    pairs = chips // group
    for index in range(group):
        term = lax.dot_general(
            mate[index], offdiag, (((0,), (0,)), ((), ())), preferred_element_type=jnp.float32
        )
        terms[index * pairs : (index + 1) * pairs] = term.reshape(pairs, *terms.shape[1:])

    pair_copy = pltpu.make_async_remote_copy(
        src_ref=terms.at[:, 1 - core],
        dst_ref=pair_buf,
        send_sem=pair_send,
        recv_sem=pair_recv,
        device_id={"row": partner},
        device_id_type=MESH,
    )
    launch(pair_copy)
    pair_copy.wait_recv()
    sums[...] = terms[:, core] + pair_buf[...]
    red_copies = []
    for step in range(1, chips):
        target = (chip + step) % chips
        copy = pltpu.make_async_remote_copy(
            src_ref=sums.at[target],
            dst_ref=red_buf.at[chip],
            send_sem=red_send.at[step],
            recv_sem=red_recv.at[step],
            device_id={"row": 2 * target + core},
            device_id_type=MESH,
        )
        launch(copy)
        red_copies.append(copy)
    own_diag.wait()
    result = sums[chip]
    for step in range(1, chips):
        red_copies[step - 1].wait_recv()
        result += red_buf[(chip + chips - step) % chips]
    out_ref[...] = diag_ref[...] - result

    for cond, copy in pending:
        if cond is None:
            copy.wait_send()
        else:
            pl.when(cond)(copy.wait_send)


def write_out(off_ref, diag_ref, off_out, diag_out, sem):
    first = pltpu.make_async_copy(off_ref, off_out, sem.at[0])
    second = pltpu.make_async_copy(diag_ref, diag_out, sem.at[1])
    first.start()
    second.start()
    first.wait()
    second.wait()


def shards(rows, cols, inverse_rows, panel_rows, diag_inverse, pattern):
    height, half = panel_rows.shape
    chunk = diag_inverse.shape[0]
    group = rows * chunk // half
    chips = rows // 2
    dma = pltpu.SemaphoreType.DMA
    vmem = pl.BlockSpec(memory_space=pltpu.VMEM)
    hbm = pl.BlockSpec(memory_space=pltpu.HBM)
    operands = (pattern, inverse_rows, panel_rows, diag_inverse)
    offdiag, diag_block = pl.pallas_call(
        functools.partial(kernel, rows, cols, group),
        out_shape=(
            jax.ShapeDtypeStruct((height, half), jnp.bfloat16),
            jax.ShapeDtypeStruct((chunk, half), jnp.float32),
        ),
        in_specs=[hbm, hbm, hbm, hbm],
        out_specs=(vmem, vmem),
        scratch_shapes=[
            pltpu.SMEM(pattern.shape, jnp.int32),
            pltpu.VMEM(diag_inverse.shape, jnp.float32),
            pltpu.VMEM((cols, *inverse_rows.shape), jnp.bfloat16),
            pltpu.VMEM((rows, height, half), jnp.bfloat16),
            pltpu.VMEM((group, height, half), jnp.bfloat16),
            pltpu.VMEM((chips, 2, chunk, half), jnp.float32),
            pltpu.VMEM((chips, chunk, half), jnp.float32),
            pltpu.VMEM((chips, chunk, half), jnp.float32),
            pltpu.VMEM((chips, chunk, half), jnp.float32),
            dma((5,)),
            dma((rows, SPLIT, 4)),
            dma((rows, SPLIT)),
            dma((cols,)),
            dma((cols,)),
            dma((group,)),
            dma((group,)),
            dma,
            dma,
            dma((chips,)),
            dma((chips,)),
        ],
        compiler_params=pltpu.CompilerParams(
            collective_id=0, has_side_effects=True, vmem_limit_bytes=48 * 1024 * 1024
        ),
    )(*(pltpu.with_memory_space_constraint(given, pltpu.HBM) for given in operands))
    return pl.pallas_call(
        write_out,
        out_shape=(
            jax.ShapeDtypeStruct((height, half), jnp.bfloat16),
            jax.ShapeDtypeStruct((chunk, half), jnp.float32),
        ),
        in_specs=[vmem, vmem],
        out_specs=(hbm, hbm),
        scratch_shapes=[dma((2,))],
        compiler_params=pltpu.CompilerParams(vmem_limit_bytes=1024 * 1024),
    )(offdiag, diag_block)


def solution(mesh):
    placed = (P("row", "col"), P("row", "col"), P("row", "col"), P())
    return jax.shard_map(
        functools.partial(shards, mesh.shape["row"], mesh.shape["col"]),
        mesh=mesh,
        in_specs=placed,
        out_specs=(P("row", "col"), P("row", "col")),
        check_vma=False,
    )
```

```python
import functools

import jax
import jax.numpy as jnp
from jax import lax
from jax.experimental import pallas as pl
from jax.experimental.pallas import tpu as pltpu
from jax.sharding import PartitionSpec as P

MESH = pl.DeviceIdType.MESH


def kernel(
    rows, cols, group,
    pattern_hbm, inv_ref, pan_ref, diag_hbm,
    off_ref, out_ref,
    pattern_ref, diag_ref, inv_buf, pan_buf, mate, off_far, off_in, terms, red_buf,
    local_sem, own_send, fwd_send, pan_recv, inv_send, inv_recv, mate_send, mate_recv,
    off_send, off_recv, red_send, red_recv,
):
    row = lax.axis_index("row")
    col = lax.axis_index("col")
    core = row % 2
    side = (row // 2) % 2
    layer = row // 4
    layers = rows // 4
    partner = row + 1 - 2 * core
    across = row + 2 - 4 * side
    place = col % group
    supernode = col // group
    height, half = pan_ref.shape
    quarter = half // 2

    def lanes(which):
        return pl.ds(pl.multiple_of(which * quarter, quarter), quarter)

    near, other = lanes(core), lanes(1 - core)

    local = [
        pltpu.make_async_copy(src, dst, local_sem.at[index])
        for index, (src, dst) in enumerate(
            [
                (pattern_hbm, pattern_ref),
                (diag_hbm, diag_ref),
                (pan_ref, mate.at[place, 0]),
                (pan_ref.at[:, near], pan_buf.at[row]),
                (inv_ref, inv_buf.at[col, 0]),
            ]
        )
    ]
    for copy in local:
        copy.start()

    barrier = pltpu.get_barrier_semaphore()

    def greet(**where):
        pl.semaphore_signal(barrier, inc=1, device_id=where, device_id_type=MESH)

    greet(row=partner)
    for base in (row, partner):
        greet(row=base + 2 - 4 * side)
        for step in range(1, layers):
            greet(row=(base + 4 * step) % rows)
    for step in range(1, cols):
        greet(col=(col + step) % cols)
    pl.semaphore_wait(barrier, 2 * layers + cols)

    pending = []

    def launch(copy, cond=None):
        if cond is None:
            copy.start()
        else:
            pl.when(cond)(copy.start)
        pending.append((cond, copy))
        return copy

    def remote(src, dst, send, recv, **where):
        return pltpu.make_async_remote_copy(
            src_ref=src,
            dst_ref=dst,
            send_sem=send,
            recv_sem=recv,
            device_id=where,
            device_id_type=MESH,
        )

    def own_panel(slot, part, target):
        return remote(
            pan_ref.at[:, part], pan_buf.at[row], own_send.at[slot], pan_recv.at[row], row=target
        )

    def passed_on(source):
        return remote(
            pan_buf.at[source], pan_buf.at[source], fwd_send.at[source], pan_recv.at[source],
            row=across,
        )

    sides = ((0, near, row), (1, other, partner))
    for slot, part, base in sides:
        launch(own_panel(slot, part, base + 2 - 4 * side))
    for far in range(1, layers):
        for slot, part, base in sides:
            slot = 4 * far + 2 * slot
            launch(own_panel(slot, part, base + 4 * far), layer < layers - far)
            launch(own_panel(slot + 1, part, base - 4 * far), layer >= far)
    launch(own_panel(2, other, partner))

    inv_copies, mate_copies = [], []
    for step in range(1, cols):
        inv_copies.append(
            launch(
                remote(
                    inv_ref, inv_buf.at[col, 0], inv_send.at[step, 0], inv_recv.at[step, 0],
                    col=(col + step) % cols,
                )
            )
        )
    for step in range(1, group):
        mate_copies.append(
            launch(
                remote(
                    pan_ref, mate.at[place, 0], mate_send.at[step, 0], mate_recv.at[step, 0],
                    col=supernode * group + (place + step) % group,
                )
            )
        )

    def share_inv(step):
        owner = (col + cols - step) % cols
        return remote(
            inv_buf.at[owner, 0] if step else inv_ref, inv_buf.at[owner, 1],
            inv_send.at[step, 1], inv_recv.at[step, 1], row=partner,
        )

    def share_mate(step):
        owner = (place + group - step) % group
        return remote(
            mate.at[owner, 0] if step else pan_ref, mate.at[owner, 1],
            mate_send.at[step, 1], mate_recv.at[step, 1], row=partner,
        )

    launch(share_inv(0))
    launch(share_mate(0))

    def arrive(source, cond, onward):
        if cond is None:
            passed_on(source).wait_recv()
        else:
            pl.when(cond)(passed_on(source).wait_recv)
        if onward:
            launch(passed_on(source), cond)

    for far in range(1, layers):
        for base in (row, partner):
            arrive(base - 4 * far, layer >= far, True)
            arrive(base + 4 * far, layer < layers - far, True)
    for step in range(1, cols):
        inv_copies[step - 1].wait_recv()
        launch(share_inv(step))
    for step in range(1, group):
        mate_copies[step - 1].wait_recv()
        launch(share_mate(step))
    arrive(partner, None, False)
    for base in (across, partner + 2 - 4 * side):
        arrive(base, None, False)
        for far in range(1, layers):
            arrive(base - 4 * far, layer >= far, False)
            arrive(base + 4 * far, layer < layers - far, False)
    for copy in local:
        copy.wait()
    for step in range(cols):
        share_inv(step).wait_recv()
    for step in range(group):
        share_mate(step).wait_recv()

    per_col = rows // cols
    total = jnp.zeros((2 * height, quarter), jnp.float32)
    for owner in range(cols):
        parts = []
        for index in range(per_col):
            block = inv_buf[owner, :, :, index * height : (index + 1) * height]
            block = block.reshape(2 * height, height)
            live = pattern_ref[supernode, owner * per_col + index] > 0
            parts.append(jnp.where(live, block, jnp.zeros_like(block)))
        panel = pan_buf[owner * per_col : (owner + 1) * per_col].reshape(-1, quarter)
        total += jnp.dot(
            jnp.concatenate(parts, axis=1), panel, preferred_element_type=jnp.float32
        )

    def kept(sums, which):
        live = pattern_ref[supernode, which] > 0
        return jnp.where(live, -sums, jnp.zeros_like(sums)).astype(jnp.bfloat16)

    off_own = kept(total[:height], row)
    off_other = kept(total[height:], partner)
    off_far[...] = off_other
    offdiag = jnp.concatenate([off_own, off_other], axis=0)
    span = rows // group
    for index in range(group):
        left = mate[index].reshape(2 * height, half)
        term = lax.dot_general(
            left, offdiag, (((0,), (0,)), ((), ())), preferred_element_type=jnp.float32
        )
        terms[index * span : (index + 1) * span] = term.reshape(span, *terms.shape[1:])

    red_copies = {}
    order = sorted(range(1, rows), key=lambda step: -min(step, rows - step))
    for step in order:
        target = (row + step) % rows
        red_copies[step] = launch(
            remote(
                terms.at[target], red_buf.at[row], red_send.at[step], red_recv.at[step],
                row=target,
            )
        )
    off_copy = launch(remote(off_far, off_in, off_send, off_recv, row=partner))
    off_ref[:, near] = off_own
    off_copy.wait_recv()
    off_ref[:, other] = off_in[...]
    results = [terms[row], None]
    for step in reversed(order):
        red_copies[step].wait_recv()
        piece = red_buf[(row + rows - step) % rows]
        which = step % 2
        results[which] = piece if results[which] is None else results[which] + piece
    out_ref[:, near] = diag_ref[:, near] - results[0]
    out_ref[:, other] = diag_ref[:, other] - results[1]

    for cond, copy in pending:
        if cond is None:
            copy.wait_send()
        else:
            pl.when(cond)(copy.wait_send)


def write_out(off_ref, diag_ref, off_out, diag_out, sem):
    first = pltpu.make_async_copy(off_ref, off_out, sem.at[0])
    second = pltpu.make_async_copy(diag_ref, diag_out, sem.at[1])
    first.start()
    second.start()
    first.wait()
    second.wait()


def shards(rows, cols, inverse_rows, panel_rows, diag_inverse, pattern):
    height, half = panel_rows.shape
    chunk = diag_inverse.shape[0]
    group = rows * chunk // half
    dma = pltpu.SemaphoreType.DMA
    vmem = pl.BlockSpec(memory_space=pltpu.VMEM)
    hbm = pl.BlockSpec(memory_space=pltpu.HBM)
    operands = (pattern, inverse_rows, panel_rows, diag_inverse)
    offdiag, diag_block = pl.pallas_call(
        functools.partial(kernel, rows, cols, group),
        out_shape=(
            jax.ShapeDtypeStruct((height, half), jnp.bfloat16),
            jax.ShapeDtypeStruct((chunk, half), jnp.float32),
        ),
        in_specs=[hbm, hbm, hbm, hbm],
        out_specs=(vmem, vmem),
        scratch_shapes=[
            pltpu.SMEM(pattern.shape, jnp.int32),
            pltpu.VMEM(diag_inverse.shape, jnp.float32),
            pltpu.VMEM((cols, 2, *inverse_rows.shape), jnp.bfloat16),
            pltpu.VMEM((rows, height, half // 2), jnp.bfloat16),
            pltpu.VMEM((group, 2, height, half), jnp.bfloat16),
            pltpu.VMEM((height, half // 2), jnp.bfloat16),
            pltpu.VMEM((height, half // 2), jnp.bfloat16),
            pltpu.VMEM((rows, chunk, half // 2), jnp.float32),
            pltpu.VMEM((rows, chunk, half // 2), jnp.float32),
            dma((5,)),
            dma((rows,)),
            dma((rows,)),
            dma((rows,)),
            dma((cols, 2)),
            dma((cols, 2)),
            dma((group, 2)),
            dma((group, 2)),
            dma,
            dma,
            dma((rows,)),
            dma((rows,)),
        ],
        compiler_params=pltpu.CompilerParams(
            collective_id=0, has_side_effects=True, vmem_limit_bytes=48 * 1024 * 1024
        ),
    )(*(pltpu.with_memory_space_constraint(given, pltpu.HBM) for given in operands))
    return pl.pallas_call(
        write_out,
        out_shape=(
            jax.ShapeDtypeStruct((height, half), jnp.bfloat16),
            jax.ShapeDtypeStruct((chunk, half), jnp.float32),
        ),
        in_specs=[vmem, vmem],
        out_specs=(hbm, hbm),
        scratch_shapes=[dma((2,))],
        compiler_params=pltpu.CompilerParams(vmem_limit_bytes=1024 * 1024),
    )(offdiag, diag_block)


def solution(mesh):
    placed = (P("row", "col"), P("row", "col"), P("row", "col"), P())
    return jax.shard_map(
        functools.partial(shards, mesh.shape["row"], mesh.shape["col"]),
        mesh=mesh,
        in_specs=placed,
        out_specs=(P("row", "col"), P("row", "col")),
        check_vma=False,
    )
```

```python
import functools

import jax
import jax.numpy as jnp
from jax import lax
from jax.experimental import pallas as pl
from jax.experimental.pallas import tpu as pltpu
from jax.sharding import PartitionSpec as P

MESH = pl.DeviceIdType.MESH


def kernel(
    rows, cols, group,
    pattern_hbm, inv_ref, pan_ref, diag_hbm,
    off_ref, out_ref,
    pattern_ref, diag_ref, inv_buf, pan_buf, mate, off_far, off_in, terms, red_buf,
    local_sem, own_send, fwd_send, pan_recv, inv_send, inv_recv, mate_send, mate_recv,
    off_send, off_recv, red_send, red_recv,
):
    row = lax.axis_index("row")
    col = lax.axis_index("col")
    core = row % 2
    side = (row // 2) % 2
    layer = row // 4
    layers = rows // 4
    partner = row + 1 - 2 * core
    across = row + 2 - 4 * side
    place = col % group
    supernode = col // group
    height, half = pan_ref.shape
    quarter = half // 2

    def lanes(which):
        return pl.ds(pl.multiple_of(which * quarter, quarter), quarter)

    near, other = lanes(core), lanes(1 - core)

    local = [
        pltpu.make_async_copy(src, dst, local_sem.at[index])
        for index, (src, dst) in enumerate(
            [
                (pattern_hbm, pattern_ref),
                (diag_hbm, diag_ref),
                (pan_ref, mate.at[place, 0]),
                (pan_ref.at[:, near], pan_buf.at[row]),
                (inv_ref, inv_buf.at[col, 0]),
            ]
        )
    ]
    for copy in local:
        copy.start()

    barrier = pltpu.get_barrier_semaphore()

    def greet(**where):
        pl.semaphore_signal(barrier, inc=1, device_id=where, device_id_type=MESH)

    greet(row=partner)
    for base in (row, partner):
        greet(row=base + 2 - 4 * side)
        for step in range(1, layers):
            greet(row=(base + 4 * step) % rows)
    for step in range(1, cols):
        greet(col=(col + step) % cols)
    pl.semaphore_wait(barrier, 2 * layers + cols)

    pending = []

    def launch(copy, cond=None):
        if cond is None:
            copy.start()
        else:
            pl.when(cond)(copy.start)
        pending.append((cond, copy))
        return copy

    def remote(src, dst, send, recv, **where):
        return pltpu.make_async_remote_copy(
            src_ref=src,
            dst_ref=dst,
            send_sem=send,
            recv_sem=recv,
            device_id=where,
            device_id_type=MESH,
        )

    def own_panel(slot, part, target):
        return remote(
            pan_ref.at[:, part], pan_buf.at[row], own_send.at[slot], pan_recv.at[row], row=target
        )

    def passed_on(source):
        return remote(
            pan_buf.at[source], pan_buf.at[source], fwd_send.at[source], pan_recv.at[source],
            row=across,
        )

    sides = ((0, near, row), (1, other, partner))
    for slot, part, base in sides:
        launch(own_panel(slot, part, base + 2 - 4 * side))
    for far in range(1, layers):
        for slot, part, base in sides:
            slot = 4 * far + 2 * slot
            launch(own_panel(slot, part, base + 4 * far), layer < layers - far)
            launch(own_panel(slot + 1, part, base - 4 * far), layer >= far)
    launch(own_panel(2, other, partner))

    inv_copies, mate_copies = [], []
    for step in range(1, cols):
        inv_copies.append(
            launch(
                remote(
                    inv_ref, inv_buf.at[col, 0], inv_send.at[step, 0], inv_recv.at[step, 0],
                    col=(col + step) % cols,
                )
            )
        )
    for step in range(1, group):
        mate_copies.append(
            launch(
                remote(
                    pan_ref, mate.at[place, 0], mate_send.at[step, 0], mate_recv.at[step, 0],
                    col=supernode * group + (place + step) % group,
                )
            )
        )

    def share_inv(step):
        owner = (col + cols - step) % cols
        return remote(
            inv_buf.at[owner, 0] if step else inv_ref, inv_buf.at[owner, 1],
            inv_send.at[step, 1], inv_recv.at[step, 1], row=partner,
        )

    def share_mate(step):
        owner = (place + group - step) % group
        return remote(
            mate.at[owner, 0] if step else pan_ref, mate.at[owner, 1],
            mate_send.at[step, 1], mate_recv.at[step, 1], row=partner,
        )

    launch(share_inv(0))
    launch(share_mate(0))

    def arrive(source, cond, onward):
        if cond is None:
            passed_on(source).wait_recv()
        else:
            pl.when(cond)(passed_on(source).wait_recv)
        if onward:
            launch(passed_on(source), cond)

    for far in range(1, layers):
        for base in (row, partner):
            arrive(base - 4 * far, layer >= far, True)
            arrive(base + 4 * far, layer < layers - far, True)
    for step in range(1, cols):
        inv_copies[step - 1].wait_recv()
        launch(share_inv(step))
    for step in range(1, group):
        mate_copies[step - 1].wait_recv()
        launch(share_mate(step))
    arrive(partner, None, False)
    for base in (across, partner + 2 - 4 * side):
        arrive(base, None, False)
        for far in range(1, layers):
            arrive(base - 4 * far, layer >= far, False)
            arrive(base + 4 * far, layer < layers - far, False)
    for copy in local:
        copy.wait()
    for step in range(cols):
        share_inv(step).wait_recv()
    for step in range(group):
        share_mate(step).wait_recv()

    per_col = rows // cols
    total = jnp.zeros((2 * height, quarter), jnp.float32)
    for owner in range(cols):
        parts = []
        for index in range(per_col):
            block = inv_buf[owner, :, :, index * height : (index + 1) * height]
            block = block.reshape(2 * height, height)
            live = pattern_ref[supernode, owner * per_col + index] > 0
            parts.append(jnp.where(live, block, jnp.zeros_like(block)))
        panel = pan_buf[owner * per_col : (owner + 1) * per_col].reshape(-1, quarter)
        total += jnp.dot(
            jnp.concatenate(parts, axis=1), panel, preferred_element_type=jnp.float32
        )

    def kept(sums, which):
        live = pattern_ref[supernode, which] > 0
        return jnp.where(live, -sums, jnp.zeros_like(sums)).astype(jnp.bfloat16)

    off_own = kept(total[:height], row)
    off_other = kept(total[height:], partner)
    off_far[...] = off_other
    offdiag = jnp.concatenate([off_own, off_other], axis=0)
    span = rows // group
    for index in range(group):
        left = mate[index].reshape(2 * height, half)
        term = lax.dot_general(
            left, offdiag, (((0,), (0,)), ((), ())), preferred_element_type=jnp.float32
        )
        terms[index * span : (index + 1) * span] = term.reshape(span, *terms.shape[1:])

    red_copies = {}
    order = sorted(range(1, rows), key=lambda step: min(step, rows - step))
    for step in order:
        target = (row + step) % rows
        red_copies[step] = launch(
            remote(
                terms.at[target], red_buf.at[row], red_send.at[step], red_recv.at[step],
                row=target,
            )
        )
    off_copy = launch(remote(off_far, off_in, off_send, off_recv, row=partner))
    off_ref[:, near] = off_own
    off_copy.wait_recv()
    off_ref[:, other] = off_in[...]
    results = [terms[row], None]
    for step in reversed(order):
        red_copies[step].wait_recv()
        piece = red_buf[(row + rows - step) % rows]
        which = step % 2
        results[which] = piece if results[which] is None else results[which] + piece
    out_ref[:, near] = diag_ref[:, near] - results[0]
    out_ref[:, other] = diag_ref[:, other] - results[1]

    for cond, copy in pending:
        if cond is None:
            copy.wait_send()
        else:
            pl.when(cond)(copy.wait_send)


def write_out(off_ref, diag_ref, off_out, diag_out, sem):
    first = pltpu.make_async_copy(off_ref, off_out, sem.at[0])
    second = pltpu.make_async_copy(diag_ref, diag_out, sem.at[1])
    first.start()
    second.start()
    first.wait()
    second.wait()


def shards(rows, cols, inverse_rows, panel_rows, diag_inverse, pattern):
    height, half = panel_rows.shape
    chunk = diag_inverse.shape[0]
    group = rows * chunk // half
    dma = pltpu.SemaphoreType.DMA
    vmem = pl.BlockSpec(memory_space=pltpu.VMEM)
    hbm = pl.BlockSpec(memory_space=pltpu.HBM)
    operands = (pattern, inverse_rows, panel_rows, diag_inverse)
    offdiag, diag_block = pl.pallas_call(
        functools.partial(kernel, rows, cols, group),
        out_shape=(
            jax.ShapeDtypeStruct((height, half), jnp.bfloat16),
            jax.ShapeDtypeStruct((chunk, half), jnp.float32),
        ),
        in_specs=[hbm, hbm, hbm, hbm],
        out_specs=(vmem, vmem),
        scratch_shapes=[
            pltpu.SMEM(pattern.shape, jnp.int32),
            pltpu.VMEM(diag_inverse.shape, jnp.float32),
            pltpu.VMEM((cols, 2, *inverse_rows.shape), jnp.bfloat16),
            pltpu.VMEM((rows, height, half // 2), jnp.bfloat16),
            pltpu.VMEM((group, 2, height, half), jnp.bfloat16),
            pltpu.VMEM((height, half // 2), jnp.bfloat16),
            pltpu.VMEM((height, half // 2), jnp.bfloat16),
            pltpu.VMEM((rows, chunk, half // 2), jnp.float32),
            pltpu.VMEM((rows, chunk, half // 2), jnp.float32),
            dma((5,)),
            dma((rows,)),
            dma((rows,)),
            dma((rows,)),
            dma((cols, 2)),
            dma((cols, 2)),
            dma((group, 2)),
            dma((group, 2)),
            dma,
            dma,
            dma((rows,)),
            dma((rows,)),
        ],
        compiler_params=pltpu.CompilerParams(
            collective_id=0, has_side_effects=True, vmem_limit_bytes=48 * 1024 * 1024
        ),
    )(*(pltpu.with_memory_space_constraint(given, pltpu.HBM) for given in operands))
    return pl.pallas_call(
        write_out,
        out_shape=(
            jax.ShapeDtypeStruct((height, half), jnp.bfloat16),
            jax.ShapeDtypeStruct((chunk, half), jnp.float32),
        ),
        in_specs=[vmem, vmem],
        out_specs=(hbm, hbm),
        scratch_shapes=[dma((2,))],
        compiler_params=pltpu.CompilerParams(vmem_limit_bytes=1024 * 1024),
    )(offdiag, diag_block)


def solution(mesh):
    placed = (P("row", "col"), P("row", "col"), P("row", "col"), P())
    return jax.shard_map(
        functools.partial(shards, mesh.shape["row"], mesh.shape["col"]),
        mesh=mesh,
        in_specs=placed,
        out_specs=(P("row", "col"), P("row", "col")),
        check_vma=False,
    )
```
